256 devices in a mesh: mem: 4 (over y), tile: 32 (over x, z_hi, core), grp: 2 (over z_lo).
Axes of the slice: x: 4, y: 4, z: 8 (z_hi: 4, z_lo: 2; z = z_hi * 2 + z_lo), core: 2. Of those that a mesh axis runs over, the one named last changes fastest.
Arguments:
- members: float32 [3, 128, 512, 512], P(None, 'mem', ('tile', 'grp')), may hold values from -0.6 to 0.6
- obs_cells: int32 [64, 4, 1024], P(('tile', 'grp'), 'mem'), may hold values from 0 to 1023
- obs_count: int32 [64, 4], P(('tile', 'grp'), 'mem'), may hold values from 128 to 1024, as said below
- obs_values: float32 [64, 4, 1024], P(('tile', 'grp'), 'mem'), may hold values from -0.6 to 0.6
- obs_error: float32 [64, 4, 1024], P(('tile', 'grp'), 'mem'), may hold values from 0.03 to 0.3
- obs_noise: float32 [64, 4, 1024, 128], P(('tile', 'grp'), 'mem'), may hold values from -6 to 6
Outputs:
- analysis: bfloat16 [3, 128, 512, 512], P(None, None, ('tile', 'grp'), 'mem')
The draws below stay inside these ranges and needn't reach their ends.
Inputs may be any that keep to these rules, and one draw needn't show every extreme that they name: `obs_count`: a multiple of 128; some tile has exactly 1024 live slots in every draw.
All inputs are finite; a program needn't handle non-finite values.
Results may differ from the reference program's by a relative error of at most 0.0058.
Values may be sent and summed in bfloat16 or wider, within the bound.
No kernel may reach another device: no remote copies, remote signals or barrier semaphores. Data moves between devices by JAX's collectives and lax.ppermute only.
A program may use at most 64 MiB of HBM per device.

```python
import math
import jax
import jax.numpy as jnp
from jax import lax

STRIP_LINES = 8
DOMAIN_VERTICALS = 512
STEPS = 4
OBS_CAP = 1024
REALIZATION_NUM = 128
DOMAIN_LINES = 512
PATCHES_SOUTHWARD = 64
PATCHES_EASTWARD = 4
PATCH_BREADTH = 128
PATCH_POINTS = 1024


def draw_obs_count(key, part):
    key_one, key_two, key_three = jax.random.split(jax.random.fold_in(key, 17), 3)
    blocks_most = OBS_CAP // 128
    factor_one = jax.random.randint(key_one, (PATCHES_SOUTHWARD, PATCHES_EASTWARD), 0, blocks_most)
    factor_two = jax.random.randint(key_two, (PATCHES_SOUTHWARD, PATCHES_EASTWARD), 0, blocks_most)
    block_count = 1 + factor_one * factor_two // (blocks_most - 1)
    position = jax.random.randint(key_three, (), 0, PATCHES_SOUTHWARD * PATCHES_EASTWARD)
    flattened = block_count.reshape(-1).at[position].set(blocks_most)
    return (flattened * 128).reshape(PATCHES_SOUTHWARD, PATCHES_EASTWARD).astype(jnp.int32)


def touch_ends(entries, key, smallest, largest):
    longest = entries.shape.index(max(entries.shape))
    spots = []
    for shift in (0, 1):
        where = [jax.random.randint(jax.random.fold_in(key, axis), (), 0, length) for axis, length in enumerate(entries.shape)]
        where[longest] = (where[longest] + shift) % entries.shape[longest]
        spots.append(tuple(where))
    return entries.at[spots[0]].set(smallest).at[spots[1]].set(largest)


def steps_of(own_key, dims, pieces, smallest, largest):
    def one(dim, parts):
        steps = jax.random.uniform(jax.random.fold_in(jax.random.fold_in(own_key, 6), dim), (parts,), jnp.float32, smallest / len(pieces), largest / len(pieces))
        return jnp.repeat(jnp.exp(steps), dims[dim] // parts).reshape((-1,) + (1,) * (len(dims) - dim - 1))

    gain = one(*pieces[0])
    for cut in pieces[1:]:
        gain = gain * one(*cut)
    return gain


def centred(key, extent, width, most, cuts=(), held_as=jnp.bfloat16):
    factor_of = steps_of(key, extent, cuts, -0.22, 0.18) if cuts else 1.0
    values = jax.random.normal(key, extent, jnp.float32) * width * factor_of
    return jnp.minimum(jnp.maximum(values, -most), most).astype(held_as)


def setup_inputs(seed: int = 0) -> dict:
    seeds = jax.random.split(jax.random.key(seed), 7)
    members = centred(seeds[0], (3, REALIZATION_NUM, DOMAIN_LINES, DOMAIN_VERTICALS), 0.1, 0.6, ((1, 4), (2, 64)), jnp.float32)
    obs_cells = touch_ends(jax.random.randint(seeds[1], (PATCHES_SOUTHWARD, PATCHES_EASTWARD, OBS_CAP), 0, PATCH_POINTS), jax.random.fold_in(seeds[1], 1), 0, PATCH_POINTS - 1).astype(jnp.int32)
    obs_count = draw_obs_count(jax.random.fold_in(seeds[6], 71), 0)
    obs_values = centred(seeds[3], (PATCHES_SOUTHWARD, PATCHES_EASTWARD, OBS_CAP), 0.1, 0.6, ((0, 64), (1, 4)), jnp.float32)
    obs_error = jnp.clip(jnp.exp(math.log(0.3) - 2.3025852 * jax.random.uniform(seeds[4], (PATCHES_SOUTHWARD, PATCHES_EASTWARD, OBS_CAP), jnp.float32) ** steps_of(seeds[4], (PATCHES_SOUTHWARD, PATCHES_EASTWARD, OBS_CAP), ((0, 64), (1, 4)), -0.2, 0.2)), 0.03, 0.3)
    obs_noise = centred(seeds[5], (PATCHES_SOUTHWARD, PATCHES_EASTWARD, OBS_CAP, REALIZATION_NUM), 1.0, 6.0, ((0, 64), (1, 4)), jnp.float32)
    return dict(members=members, obs_cells=obs_cells, obs_count=obs_count, obs_values=obs_values, obs_error=obs_error, obs_noise=obs_noise)


courant = 0.3
gravity = 1.0
coriolis = 0.1

def beside_all(field_e, field_w, field_n, field_s):
    return 0.25 * (field_e + field_w + field_n + field_s)

def advance(padded):
    height = padded[0]
    zonal = padded[1]
    meridional = padded[2]
    height_e, height_w, height_mid = (height[:, 2:, :], height[:, :-2, :], height[:, 1:-1, :])
    zonal_e, zonal_w, zonal_mid = (zonal[:, 2:, :], zonal[:, :-2, :], zonal[:, 1:-1, :])
    merid_e, merid_w, merid_mid = (meridional[:, 2:, :], meridional[:, :-2, :], meridional[:, 1:-1, :])
    height_n, height_s = (jnp.roll(height_mid, -1, axis=2), jnp.roll(height_mid, 1, axis=2))
    zonal_n, zonal_s = (jnp.roll(zonal_mid, -1, axis=2), jnp.roll(zonal_mid, 1, axis=2))
    merid_n, merid_s = (jnp.roll(merid_mid, -1, axis=2), jnp.roll(merid_mid, 1, axis=2))
    new_height = beside_all(height_e, height_w, height_n, height_s) - courant * ((1.0 + height_e) * zonal_e - (1.0 + height_w) * zonal_w) - courant * ((1.0 + height_n) * merid_n - (1.0 + height_s) * merid_s)
    new_zonal = beside_all(zonal_e, zonal_w, zonal_n, zonal_s) - courant * (0.5 * zonal_e * zonal_e + gravity * height_e - (0.5 * zonal_w * zonal_w + gravity * height_w)) - courant * merid_mid * (zonal_n - zonal_s) + coriolis * merid_mid
    new_merid = beside_all(merid_e, merid_w, merid_n, merid_s) - courant * (0.5 * merid_n * merid_n + gravity * height_n - (0.5 * merid_s * merid_s + gravity * height_s)) - courant * zonal_mid * (merid_e - merid_w) - coriolis * zonal_mid
    return jnp.stack([new_height, new_zonal, new_merid])

def predict_realization_group(fluid_condition):
    for step_index in range(STEPS):
        padded = jnp.concatenate([fluid_condition[:, :, -1:, :], fluid_condition, fluid_condition[:, :, :1, :]], axis=2)
        fluid_condition = advance(padded)
    return fluid_condition

def analyse(fields, cell_ids, live_count, obs_vals, obs_std, perturb):
    ens_size = fields.shape[1]
    states = fields.astype(jnp.float32)
    spread = states - jnp.mean(states, axis=1, keepdims=True)
    observed = jnp.take(states[0], cell_ids, axis=1)
    obs_spread = observed - jnp.mean(observed, axis=0, keepdims=True)
    slot_ids = jnp.arange(obs_vals.shape[0], dtype=jnp.int32)
    weights = jnp.where(slot_ids < live_count, 1.0 / (obs_std * obs_std), 0.0).astype(jnp.float32)
    weighted = obs_spread * weights[None, :]
    innov = obs_vals[None, :] + obs_std[None, :] * perturb.T - observed
    gram = (ens_size - 1.0) * jnp.eye(ens_size, dtype=jnp.float32) + jnp.dot(weighted, obs_spread.T, precision=lax.Precision.HIGHEST)
    rhs_matrix = jnp.dot(weighted, innov.T, precision=lax.Precision.HIGHEST)
    factor = jnp.linalg.cholesky(gram)
    weight_matrix = jax.scipy.linalg.cho_solve((factor, True), rhs_matrix)
    update = jnp.einsum('vkc,kj->vjc', spread, weight_matrix, precision=lax.Precision.HIGHEST)
    return (states + update).astype(jnp.bfloat16)

def reference(members, obs_cells, obs_count, obs_values, obs_error, obs_noise):
    batch_size = math.gcd(REALIZATION_NUM, 16)
    realization_groups = jnp.moveaxis(members.reshape(3, REALIZATION_NUM // batch_size, batch_size, DOMAIN_LINES, DOMAIN_VERTICALS), 1, 0)
    advanced_conditions = lax.map(predict_realization_group, realization_groups)
    predict_realizations = jnp.moveaxis(advanced_conditions, 0, 1).reshape(3, REALIZATION_NUM, DOMAIN_LINES, DOMAIN_VERTICALS).astype(jnp.bfloat16)
    condition_patches = predict_realizations.reshape(3, REALIZATION_NUM, PATCHES_SOUTHWARD, STRIP_LINES, PATCHES_EASTWARD, PATCH_BREADTH).transpose(2, 4, 0, 1, 3, 5).reshape(PATCHES_SOUTHWARD * PATCHES_EASTWARD, 3, REALIZATION_NUM, PATCH_POINTS)
    results = lax.map(lambda item: analyse(*item), (condition_patches, obs_cells.reshape(PATCHES_SOUTHWARD * PATCHES_EASTWARD, OBS_CAP), obs_count.reshape(PATCHES_SOUTHWARD * PATCHES_EASTWARD), obs_values.reshape(PATCHES_SOUTHWARD * PATCHES_EASTWARD, OBS_CAP), obs_error.reshape(PATCHES_SOUTHWARD * PATCHES_EASTWARD, OBS_CAP), obs_noise.reshape(PATCHES_SOUTHWARD * PATCHES_EASTWARD, OBS_CAP, REALIZATION_NUM)))
    return results.reshape(PATCHES_SOUTHWARD, PATCHES_EASTWARD, 3, REALIZATION_NUM, STRIP_LINES, PATCH_BREADTH).transpose(2, 3, 0, 4, 1, 5).reshape(3, REALIZATION_NUM, DOMAIN_LINES, DOMAIN_VERTICALS)
```

```python
import functools

import jax
import jax.numpy as jnp
from jax import lax
from jax.experimental import pallas as pl
from jax.experimental.pallas import tpu as pltpu
from jax.sharding import PartitionSpec as P

STEPS = 4
F32 = jnp.float32
BF16 = jnp.bfloat16
HIGHEST = lax.Precision.HIGHEST
CH = 0.09
CU = 0.3
MIB = 1 << 20


def dot(a, b):
    return jnp.dot(a, b, preferred_element_type=F32, precision=HIGHEST)


def dot_t(a, b, precision=HIGHEST):
    return lax.dot_general(
        a, b, (((1,), (1,)), ((), ())), preferred_element_type=F32, precision=precision
    )


def edges_kernel(x_ref, low_ref, high_ref):
    members, cols = low_ref.shape[2:]
    for f in range(3):
        for r in range(STEPS):
            for t in range(cols // 128):
                part = pl.ds(t * 128, 128)
                for out_ref, row in ((low_ref, r), (high_ref, 8 - STEPS + r)):
                    q = x_ref[f, pl.ds(t * 8 + row, members, stride=cols // 16), :]
                    out_ref[f, r, :, part] = q.astype(BF16)


def edges(x, cols):
    members = x.shape[1] * 16 // cols
    half = members // 2
    shape = jax.ShapeDtypeStruct((3, STEPS, members, cols), BF16)
    return pl.pallas_call(
        edges_kernel,
        grid=(2,),
        in_specs=[pl.BlockSpec((3, half * cols // 16, 128), lambda i: (0, i, 0))],
        out_specs=[pl.BlockSpec((3, STEPS, half, cols), lambda i: (0, 0, i, 0))] * 2,
        out_shape=[shape, shape],
        compiler_params=pltpu.CompilerParams(vmem_limit_bytes=32 * MIB),
        cost_estimate=pl.CostEstimate(flops=x.size, bytes_accessed=x.size * 6, transcendentals=0),
        name="edges",
    )(x)


def forecast_kernel(x_ref, below_ref, above_ref, h_ref, uv_ref, ping, pong, edge):
    members, cols = below_ref.shape[2], below_ref.shape[3]
    tiles = h_ref.shape[0]
    stride = cols // 16
    for f in range(3):
        for r in range(STEPS):
            edge[f, r] = below_ref[f, r].astype(F32)
            edge[f, STEPS + r] = above_ref[f, r].astype(F32)

    def north(q):
        return pltpu.roll(q, cols - 1, axis=1)

    def south(q):
        return pltpu.roll(q, 1, axis=1)

    def group(g, _):
        first = pl.multiple_of(g * 8, 8)

        def start(f, p):
            if p < STEPS:
                q = edge[f, p, pl.ds(first, 8), :]
            elif p < STEPS + 8:
                base = pl.multiple_of(g * (8 * stride), 8 * stride) + (p - STEPS)
                q = jnp.concatenate(
                    [x_ref[f, pl.ds(base + t * 8, 8, stride=stride), :] for t in range(tiles)], axis=1
                )
            else:
                q = edge[f, p - 8, pl.ds(first, 8), :]
            return q * CH + CH if f == 0 else q * CU

        for step in range(STEPS):
            source, target = (ping, pong) if step % 2 else (pong, ping)

            def row(p):
                if step == 0:
                    h, u, v = (start(f, p) for f in range(3))
                else:
                    h, u, v = (source[f, p, pl.ds(first, 8), :] for f in range(3))
                up, um = 0.25 + u, 0.25 - u
                flux = 0.5 * (u * u) + h
                quarter = 0.25 * u
                return dict(
                    h=h, u=u, v=v, up=up, um=um,
                    he=h * um, hw=h * up, ue=quarter - flux, uw=quarter + flux,
                )

            west, mid = row(step), row(step + 1)
            for p in range(step + 1, 15 - step):
                east = row(p + 1)
                h, u, v = mid["h"], mid["u"], mid["v"]
                vp, vm = 0.25 + v, 0.25 - v
                flux = 0.5 * (v * v) + h
                quarter = 0.25 * v
                new_h = (east["he"] + west["hw"]) + (north(h * vm) + south(h * vp))
                new_u = (east["ue"] + west["uw"]) + (north(u) * vm + south(u) * vp) + 0.1 * v
                new_v = (
                    (north(quarter - flux) + south(quarter + flux))
                    + (east["v"] * mid["um"] + west["v"] * mid["up"])
                    - 0.1 * u
                )
                for f, q in enumerate((new_h, new_u, new_v)):
                    target[f, p, pl.ds(first, 8), :] = q
                west, mid = mid, east
        return 0

    lax.fori_loop(0, members // 8, group, 0)
    last = pong if STEPS % 2 == 0 else ping
    for r in range(8):
        for t in range(tiles):
            part = pl.ds(t * 128, 128)
            h_ref[t, r] = (last[0, STEPS + r, :, part] * (1.0 / CH) - 1.0).astype(BF16)
            for f in range(2):
                uv_ref[t, f, r] = (last[1 + f, STEPS + r, :, part] * (1.0 / CU)).astype(BF16)


def forecast(x, below, above, tiles):
    members, cols = below.shape[2:]
    half = members // 2
    edge_spec = pl.BlockSpec((3, STEPS, half, cols), lambda i: (0, 0, i, 0))
    return pl.pallas_call(
        forecast_kernel,
        grid=(2,),
        in_specs=[
            pl.BlockSpec((3, half * cols // 16, 128), lambda i: (0, i, 0)),
            edge_spec,
            edge_spec,
        ],
        out_specs=[
            pl.BlockSpec((tiles, 8, half, 128), lambda i: (0, 0, i, 0)),
            pl.BlockSpec((tiles, 2, 8, half, 128), lambda i: (0, 0, 0, i, 0)),
        ],
        out_shape=[
            jax.ShapeDtypeStruct((tiles, 8, members, 128), BF16),
            jax.ShapeDtypeStruct((tiles, 2, 8, members, 128), BF16),
        ],
        scratch_shapes=[
            pltpu.VMEM((3, 16, half, cols), F32),
            pltpu.VMEM((3, 16, half, cols), F32),
            pltpu.VMEM((3, 2 * STEPS, half, cols), F32),
        ],
        compiler_params=pltpu.CompilerParams(vmem_limit_bytes=40 * MIB),
        cost_estimate=pl.CostEstimate(flops=x.size * 200, bytes_accessed=x.size * 8, transcendentals=0),
        name="forecast",
    )(x, below, above)


def slots_kernel(count_ref, cells_ref, values_ref, error_ref, noise_ref, z_ref, omega_ref, lhs):
    slots = cells_ref.shape[1]
    members = noise_ref.shape[1]
    error = error_ref[...]
    live = lax.broadcasted_iota(jnp.int32, (1, slots), 1) < count_ref[0, 0]
    weight = jnp.where(live, 1.0 / (error * error), 0.0)
    rows = members + 16

    def put(at, size, cols, value):
        high = value.astype(BF16)
        rest = value - high.astype(F32)
        middle = rest.astype(BF16)
        low = (rest - middle.astype(F32)).astype(BF16)
        for k, q in enumerate((high, middle, low)):
            lhs[pl.ds(k * rows + at, size), cols] = q

    for b in range(slots // 128):
        part = pl.ds(b * 128, 128)
        lane = slice(b * 128, (b + 1) * 128)
        innovation = values_ref[:, part] + error[:, lane] * noise_ref[part, :].T
        put(0, members, part, weight[:, lane] * innovation)
    put(members, 16, pl.ds(0, slots), jnp.broadcast_to(weight, (16, slots)))
    block = 256
    cells = cells_ref[...]
    for b in range(z_ref.shape[1] // block):
        ids = lax.broadcasted_iota(jnp.int32, (block, slots), 0) + b * block
        chosen = jnp.where(ids == cells, 1.0, 0.0).astype(BF16)
        total = lax.dot_general(
            lhs[...], chosen, (((1,), (1,)), ((), ())), preferred_element_type=F32
        )
        total = total[:rows] + (total[rows : 2 * rows] + total[2 * rows :])
        part = pl.ds(b * block, block)
        z_ref[:, part] = total[:members]
        omega_ref[:, part] = total[members : members + 8]


def slots_to_cells(count, cells, values, error, noise):
    slots, members = noise.shape
    vmem = pl.BlockSpec(memory_space=pltpu.VMEM)
    return pl.pallas_call(
        slots_kernel,
        in_specs=[pl.BlockSpec(memory_space=pltpu.SMEM)] + [vmem] * 4,
        out_specs=[vmem, vmem],
        out_shape=[
            jax.ShapeDtypeStruct((members, 1024), F32),
            jax.ShapeDtypeStruct((8, 1024), F32),
        ],
        scratch_shapes=[pltpu.VMEM((3 * (members + 16), slots), BF16)],
        compiler_params=pltpu.CompilerParams(vmem_limit_bytes=32 * MIB),
        cost_estimate=pl.CostEstimate(
            flops=4 * members * slots * 1024, bytes_accessed=8 * noise.size, transcendentals=0
        ),
        name="slots_to_cells",
    )(count, cells, values, error, noise)


def weights_kernel(rank_ref, z_ref, omega_ref, p0, p1, p2, p3, w_ref, x_ref, lhs, t_ref, q_ref):
    parts = (p0, p1, p2, p3)
    size = p0.shape[1]
    members = size * len(parts)
    for s, part in enumerate(parts):
        for r in range(8):
            x_ref[pl.ds(s * size, size), pl.ds(r * 128, 128)] = part[r].astype(F32)
    x = x_ref[...]
    mean = jnp.sum(x, axis=0, keepdims=True) * (1.0 / members)
    x = x - mean
    omega = omega_ref[pl.ds(0, 1), :]
    lhs[pl.ds(0, members), :] = x * omega
    lhs[pl.ds(members, members), :] = z_ref[...] - omega * mean
    both = dot_t(lhs[...], x)
    shape = (members, members)
    down = lax.broadcasted_iota(jnp.int32, shape, 0)
    across = lax.broadcasted_iota(jnp.int32, shape, 1)
    eye = jnp.where(down == across, 1.0, 0.0)
    source = rank_ref[0, 0] + len(parts) - across // size
    source = jnp.where(source >= len(parts), source - len(parts), source)
    own = jnp.where(down == source * size + across % size, 1.0, 0.0)
    diagonal = members - 1.0
    gram = both[:members]
    rhs = both[members:] + diagonal * own
    square = dot(gram, gram)
    gram = gram + diagonal * eye
    top = jnp.sqrt(jnp.sqrt(jnp.sum(square * square)))
    low = 0.98 * diagonal
    high = 1.01 * (diagonal + top)
    inv = 1.0 / (high - low)
    z = (high + low) * inv
    alpha = (high + low - 2.0 * diagonal) * inv
    beta = 2.0 * inv
    less = gram - diagonal * eye
    t1 = alpha * eye - beta * less
    t2 = (2.0 * alpha * alpha - 1.0) * eye - (4.0 * alpha * beta) * less + (2.0 * beta * beta) * square
    z2 = 2.0 * z * z - 1.0
    t_ref[...] = t2
    q_ref[...] = (2.0 / (high + low)) * (2.0 * z / z2) * (z * eye + t1)

    def double(t):
        cheb, q = t_ref[...], q_ref[...]
        after = 2.0 * t * t - 1.0
        q_ref[...] = (2.0 * t / after) * (t * q + dot(q, cheb))
        t_ref[...] = 2.0 * dot(cheb, cheb) - eye
        return after

    lax.while_loop(lambda t: t < 3000.0, double, z2)
    inverse = q_ref[...]
    w = dot(rhs, inverse)
    w = w + dot(rhs - dot(w, gram), inverse)
    high_part = w.astype(BF16)
    w_ref[:, pl.ds(0, members)] = high_part
    w_ref[:, pl.ds(members, members)] = (w - high_part.astype(F32)).astype(BF16)


def weights(rank, z, omega, parts):
    members = z.shape[0]
    vmem = pl.BlockSpec(memory_space=pltpu.VMEM)
    return pl.pallas_call(
        weights_kernel,
        in_specs=[pl.BlockSpec(memory_space=pltpu.SMEM)] + [vmem] * 6,
        out_specs=vmem,
        out_shape=jax.ShapeDtypeStruct((members, 2 * members), BF16),
        scratch_shapes=[
            pltpu.VMEM((members, 1024), F32),
            pltpu.VMEM((2 * members, 1024), F32),
            pltpu.VMEM((members, members), F32),
            pltpu.VMEM((members, members), F32),
        ],
        compiler_params=pltpu.CompilerParams(vmem_limit_bytes=32 * MIB),
        cost_estimate=pl.CostEstimate(
            flops=100 * members**3, bytes_accessed=8 * z.size, transcendentals=0
        ),
        name="weights",
    )(rank, z, omega, *parts)


def apply_kernel(w_ref, *refs):
    h_parts, uv_parts, out_ref, stage = refs[:4], refs[4:8], refs[8], refs[9]
    members = out_ref.shape[1] // 8
    w = w_ref[...]
    for f in range(3):
        for r in range(8):
            pieces = [p[r] for p in h_parts] if f == 0 else [p[f - 1, r] for p in uv_parts]
            x = jnp.concatenate(pieces + pieces, axis=0)
            stage[pl.ds(r, members, stride=8), :] = jnp.dot(w, x, preferred_element_type=F32)
        out_ref[f] = stage[...].astype(BF16)


def apply_weights(w, h_parts, uv_parts):
    members = w.shape[0]
    vmem = pl.BlockSpec(memory_space=pltpu.VMEM)
    return pl.pallas_call(
        apply_kernel,
        in_specs=[vmem] * 9,
        out_specs=vmem,
        out_shape=jax.ShapeDtypeStruct((3, members * 8, 128), BF16),
        scratch_shapes=[pltpu.VMEM((members * 8, 128), F32)],
        compiler_params=pltpu.CompilerParams(vmem_limit_bytes=32 * MIB),
        cost_estimate=pl.CostEstimate(
            flops=12 * members * members * 1024, bytes_accessed=12 * members * 1024, transcendentals=0
        ),
        name="apply_weights",
    )(w, *h_parts, *uv_parts)


def send(x, axis, shift):
    size = lax.axis_size(axis)
    return lax.ppermute(x, axis, [(i, (i + shift) % size) for i in range(size)])


def body(members, obs_cells, obs_count, obs_values, obs_error, obs_noise):
    rows = ("tile", "grp")
    fields, count, lines, cols = members.shape
    x = members.reshape(fields, count, lines, cols // 128, 128)
    x = x.transpose(0, 1, 3, 2, 4).reshape(fields, -1, 128)
    low, high = edges(x, cols)
    below = send(high, rows, 1)
    above = send(low, rows, -1)
    slots = obs_cells.shape[-1]
    z, omega = slots_to_cells(
        obs_count,
        obs_cells.reshape(1, slots),
        obs_values.reshape(1, slots),
        obs_error.reshape(1, slots),
        obs_noise.reshape(slots, -1),
    )
    size = lax.axis_size("mem")
    h, uv = forecast(x, below, above, size)
    rank = lax.axis_index("mem")

    def exchange(blocks):
        parts = []
        for shift in range(size):
            block = lax.dynamic_index_in_dim(blocks, (rank + shift) % size, 0, keepdims=False)
            parts.append(send(block, "mem", shift) if shift else block)
        return parts

    h_parts = exchange(h)
    uv_parts = exchange(uv)
    w = weights(rank.astype(jnp.int32).reshape(1, 1), z, omega, h_parts)
    out = apply_weights(w, h_parts, uv_parts)
    return out.reshape(fields, -1, lines, 128)


def solution(mesh):
    in_specs = (
        P(None, "mem", ("tile", "grp"), None),
        P(("tile", "grp"), "mem", None),
        P(("tile", "grp"), "mem"),
        P(("tile", "grp"), "mem", None),
        P(("tile", "grp"), "mem", None),
        P(("tile", "grp"), "mem", None, None),
    )
    out_specs = P(None, None, ("tile", "grp"), "mem")
    return jax.shard_map(body, mesh=mesh, in_specs=in_specs, out_specs=out_specs, check_vma=False)
```

```python
import functools

import jax
import jax.numpy as jnp
from jax import lax
from jax.experimental import pallas as pl
from jax.experimental.pallas import tpu as pltpu
from jax.sharding import PartitionSpec as P

STEPS = 4
F32 = jnp.float32
BF16 = jnp.bfloat16
HIGHEST = lax.Precision.HIGHEST
CH = 0.09
CU = 0.3
MIB = 1 << 20


def dot(a, b):
    return jnp.dot(a, b, preferred_element_type=F32, precision=HIGHEST)


def dot_t(a, b, precision=HIGHEST):
    return lax.dot_general(
        a, b, (((1,), (1,)), ((), ())), preferred_element_type=F32, precision=precision
    )


def edges_kernel(x_hbm, x_ref, first_ref, second_ref, sems):
    members, cols = first_ref.shape[2:]
    odd = lax.axis_index("grp")
    copies = [pltpu.make_async_copy(x_hbm.at[f], x_ref.at[f], sems.at[f]) for f in range(3)]
    for copy in copies:
        copy.start()
    for f in range(3):
        copies[f].wait()
        for out_ref, base in ((first_ref, STEPS * (1 - odd)), (second_ref, STEPS * odd)):
            for r in range(STEPS):
                for t in range(cols // 128):
                    q = x_ref[f, pl.ds(base + (t * 8 + r), members, stride=cols // 16), :]
                    out_ref[f, r, :, pl.ds(t * 128, 128)] = q.astype(BF16)


def edges(x, cols):
    members = x.shape[1] * 16 // cols
    shape = jax.ShapeDtypeStruct((3, STEPS, members, cols), BF16)
    return pl.pallas_call(
        edges_kernel,
        in_specs=[pl.BlockSpec(memory_space=pltpu.HBM)],
        out_specs=[pl.BlockSpec(memory_space=pltpu.VMEM)] * 3,
        out_shape=[jax.ShapeDtypeStruct(x.shape, F32), shape, shape],
        scratch_shapes=[pltpu.SemaphoreType.DMA((3,))],
        compiler_params=pltpu.CompilerParams(vmem_limit_bytes=16 * MIB),
        cost_estimate=pl.CostEstimate(flops=x.size, bytes_accessed=x.size * 6, transcendentals=0),
        name="edges",
    )(pltpu.with_memory_space_constraint(x, pltpu.HBM))


INNER = [(t, r) for t in range(STEPS) for r in range(t, 8 - t) if t or r in (0, 1, 6, 7)]


def advance_rows(load, store, rows):
    def north(q):
        return pltpu.roll(q, q.shape[1] - 1, axis=1)

    def south(q):
        return pltpu.roll(q, 1, axis=1)

    def terms(p):
        h, u, v = (load(f, p) for f in range(3))
        up, um = 0.25 + u, 0.25 - u
        flux = 0.5 * (u * u) + h
        quarter = 0.25 * u
        return dict(
            h=h, u=u, v=v, up=up, um=um,
            he=h * um, hw=h * up, ue=quarter - flux, uw=quarter + flux,
        )

    west, mid = terms(rows[0] - 1), terms(rows[0])
    for p in rows:
        east = terms(p + 1)
        h, u, v = mid["h"], mid["u"], mid["v"]
        vp, vm = 0.25 + v, 0.25 - v
        flux = 0.5 * (v * v) + h
        quarter = 0.25 * v
        store(0, p, (east["he"] + west["hw"]) + (north(h * vm) + south(h * vp)))
        store(1, p, (east["ue"] + west["uw"]) + (north(u) * vm + south(u) * vp) + 0.1 * v)
        store(
            2,
            p,
            (north(quarter - flux) + south(quarter + flux))
            + (east["v"] * mid["um"] + west["v"] * mid["up"])
            - 0.1 * u,
        )
        west, mid = mid, east


def inner_kernel(x_ref, inner_ref):
    members, cols = inner_ref.shape[2:]
    tiles, stride = cols // 128, cols // 16

    def group(g, _):
        part = pl.ds(pl.multiple_of(g * 8, 8), 8)
        base = pl.multiple_of(g * (8 * stride), 8 * stride)

        def load(f, p):
            q = jnp.concatenate(
                [x_ref[f, pl.ds(base + (t * 8 + p), 8, stride=stride), :] for t in range(tiles)],
                axis=1,
            )
            return q * CH + CH if f == 0 else q * CU

        for p in (0, 1, 6, 7):
            for f in range(3):
                inner_ref[f, INNER.index((0, p)), part, :] = load(f, p)
        for step in range(1, STEPS):

            def source(f, p):
                if step == 1:
                    return load(f, p)
                return inner_ref[f, INNER.index((step - 1, p)), part, :]

            def target(f, p, q):
                inner_ref[f, INNER.index((step, p)), part, :] = q

            advance_rows(source, target, range(step, 8 - step))
        return 0

    lax.fori_loop(0, members // 8, group, 0)


def inner_part(x, cols):
    members = x.shape[1] * 16 // cols
    vmem = pl.BlockSpec(memory_space=pltpu.VMEM)
    return pl.pallas_call(
        inner_kernel,
        in_specs=[vmem],
        out_specs=vmem,
        out_shape=jax.ShapeDtypeStruct((3, len(INNER), members, cols), F32),
        compiler_params=pltpu.CompilerParams(vmem_limit_bytes=32 * MIB),
        cost_estimate=pl.CostEstimate(flops=x.size * 50, bytes_accessed=x.size * 8, transcendentals=0),
        name="forecast_inner",
    )(x)


def side_kernel(second, plan, tiles, inner_ref, halo_ref, *refs):
    outs, (ping, pong, edge) = refs[-3 - len(plan) : -3], refs[-3:]
    before = refs[: -3 - len(plan)]
    members, cols = halo_ref.shape[2:]
    for f in range(3):
        for r in range(STEPS):
            q = halo_ref[f, r].astype(F32)
            edge[f, r] = q * CH + CH if f == 0 else q * CU

    def side(above):
        def first_row(t):
            return 8 - t if above else t - STEPS

        def group(g, _):
            part = pl.ds(pl.multiple_of(g * 8, 8), 8)
            for step in range(1, STEPS + 1):
                source_ref, target_ref = (ping, pong) if step % 2 else (pong, ping)

                def source(f, p):
                    if step - 1 <= p < 9 - step:
                        return inner_ref[f, INNER.index((step - 1, p)), part, :]
                    if step == 1:
                        return edge[f, p - 8 if above else p + STEPS, part, :]
                    return source_ref[f, p - first_row(step - 1), part, :]

                def target(f, p, q):
                    target_ref[f, p - first_row(step), part, :] = q

                advance_rows(source, target, range(first_row(step), first_row(step) + STEPS))
            return 0

        lax.fori_loop(0, members // 8, group, 0)

    from_above = lax.axis_index("grp") == (1 if second else 0)
    pl.when(from_above)(lambda: side(True))
    pl.when(jnp.logical_not(from_above))(lambda: side(False))
    last = ping if STEPS % 2 == 0 else pong
    rank = lax.axis_index("mem")
    for (shift, fields), out_ref in zip(plan, outs):
        base = out_ref.shape[1] - STEPS
        part = pl.ds(pl.multiple_of(lax.rem(rank + shift, tiles) * 128, 128), 128)
        for k, f in enumerate(fields):
            if base:
                out_ref[k, :STEPS] = before[shift][f]
            for r in range(STEPS):
                q = last[f, r, :, part]
                q = q * (1.0 / CH) - 1.0 if f == 0 else q * (1.0 / CU)
                out_ref[k, base + r] = q.astype(BF16)


def side_part(inner, halo, second, plan, tiles, before=()):
    members, cols = halo.shape[2:]
    vmem = pl.BlockSpec(memory_space=pltpu.VMEM)
    rows = [STEPS if shift == 0 or not second else 2 * STEPS for shift, _ in plan]
    return pl.pallas_call(
        functools.partial(side_kernel, second, plan, tiles),
        in_specs=[vmem] * (2 + len(before)),
        out_specs=[vmem] * len(plan),
        out_shape=[
            jax.ShapeDtypeStruct((len(fields), n, members, 128), BF16)
            for n, (_, fields) in zip(rows, plan)
        ],
        scratch_shapes=[pltpu.VMEM((3, STEPS, members, cols), F32)] * 3,
        compiler_params=pltpu.CompilerParams(vmem_limit_bytes=24 * MIB),
        cost_estimate=pl.CostEstimate(
            flops=halo.size * 160, bytes_accessed=halo.size * 16, transcendentals=0
        ),
        name="forecast_second" if second else "forecast_first",
    )(inner, halo, *before)


def slots_kernel(count_ref, cells_ref, values_ref, error_ref, noise_ref, z_ref, omega_ref, lhs):
    slots = cells_ref.shape[1]
    members = noise_ref.shape[1]
    error = error_ref[...]
    live = lax.broadcasted_iota(jnp.int32, (1, slots), 1) < count_ref[0, 0]
    weight = jnp.where(live, 1.0 / (error * error), 0.0)
    rows = members + 16

    def put(at, size, cols, value):
        high = value.astype(BF16)
        rest = value - high.astype(F32)
        middle = rest.astype(BF16)
        low = (rest - middle.astype(F32)).astype(BF16)
        for k, q in enumerate((high, middle, low)):
            lhs[pl.ds(k * rows + at, size), cols] = q

    for b in range(slots // 128):
        part = pl.ds(b * 128, 128)
        lane = slice(b * 128, (b + 1) * 128)
        innovation = values_ref[:, part] + error[:, lane] * noise_ref[part, :].T
        put(0, members, part, weight[:, lane] * innovation)
    put(members, 16, pl.ds(0, slots), jnp.broadcast_to(weight, (16, slots)))
    block = 256
    cells = cells_ref[...]
    for b in range(z_ref.shape[1] // block):
        ids = lax.broadcasted_iota(jnp.int32, (block, slots), 0) + b * block
        chosen = jnp.where(ids == cells, 1.0, 0.0).astype(BF16)
        total = lax.dot_general(
            lhs[...], chosen, (((1,), (1,)), ((), ())), preferred_element_type=F32
        )
        total = total[:rows] + (total[rows : 2 * rows] + total[2 * rows :])
        part = pl.ds(b * block, block)
        z_ref[:, part] = total[:members]
        omega_ref[:, part] = total[members : members + 8]


def slots_to_cells(count, cells, values, error, noise):
    slots, members = noise.shape
    vmem = pl.BlockSpec(memory_space=pltpu.VMEM)
    return pl.pallas_call(
        slots_kernel,
        in_specs=[pl.BlockSpec(memory_space=pltpu.SMEM)] + [vmem] * 4,
        out_specs=[vmem, vmem],
        out_shape=[
            jax.ShapeDtypeStruct((members, 1024), F32),
            jax.ShapeDtypeStruct((8, 1024), F32),
        ],
        scratch_shapes=[pltpu.VMEM((3 * (members + 16), slots), BF16)],
        compiler_params=pltpu.CompilerParams(vmem_limit_bytes=32 * MIB),
        cost_estimate=pl.CostEstimate(
            flops=4 * members * slots * 1024, bytes_accessed=8 * noise.size, transcendentals=0
        ),
        name="slots_to_cells",
    )(count, cells, values, error, noise)


def split(a):
    high = a.astype(BF16)
    return high, (a - high.astype(F32)).astype(BF16)


def half_bases():
    odd = lax.axis_index("grp")
    return STEPS * (1 - odd), STEPS * odd


def piece(refs, where, s, f, half, r):
    array, field, row = where[s][f][half]
    return refs[array][field, row + r]


def weights_kernel(where, z_ref, omega_ref, *refs):
    parts, (w_ref, x_ref, t_ref, q_ref) = refs[:-4], refs[-4:]
    devices = len(where)
    size = parts[0].shape[2]
    members = size * devices
    for half, base in enumerate(half_bases()):
        for r in range(STEPS):
            lanes = pl.ds(pl.multiple_of((base + r) * 128, 128), 128)
            for s in range(devices):
                x_ref[pl.ds(s * size, size), lanes] = piece(parts, where, s, 0, half, r).astype(F32)
    x = x_ref[...]
    mean = jnp.sum(x, axis=0, keepdims=True) * (1.0 / members)
    x = x - mean
    omega = omega_ref[pl.ds(0, 1), :]
    left_high, left_low = split(jnp.concatenate([x * omega, z_ref[...] - omega * mean], axis=0))
    high, low = split(x)
    both = dot_t(left_high, high, None) + (
        dot_t(left_high, low, None) + dot_t(left_low, high, None)
    )
    shape = (members, members)
    down = lax.broadcasted_iota(jnp.int32, shape, 0)
    across = lax.broadcasted_iota(jnp.int32, shape, 1)
    eye = jnp.where(down == across, 1.0, 0.0)
    rank = lax.axis_index("mem")
    member = lax.rem(rank + devices - across // size, devices) * size + lax.rem(across, size)
    own = jnp.where(down == member, 1.0, 0.0)
    diagonal = members - 1.0
    gram = both[:members]
    rhs = both[members:] + diagonal * own
    square = dot(gram, gram)
    gram = gram + diagonal * eye
    top = jnp.sqrt(jnp.sqrt(jnp.sum(square * square)))
    low = 0.98 * diagonal
    high = 1.01 * (diagonal + top)
    inv = 1.0 / (high - low)
    z = (high + low) * inv
    alpha = (high + low - 2.0 * diagonal) * inv
    beta = 2.0 * inv
    less = gram - diagonal * eye
    t1 = alpha * eye - beta * less
    t2 = (2.0 * alpha * alpha - 1.0) * eye - (4.0 * alpha * beta) * less + (2.0 * beta * beta) * square
    z2 = 2.0 * z * z - 1.0
    t_ref[...] = t2
    q_ref[...] = (2.0 / (high + low)) * (2.0 * z / z2) * (z * eye + t1)

    def double(t):
        cheb, q = t_ref[...], q_ref[...]
        after = 2.0 * t * t - 1.0
        q_ref[...] = (2.0 * t / after) * (t * q + dot(q, cheb))
        t_ref[...] = 2.0 * dot(cheb, cheb) - eye
        return after

    lax.while_loop(lambda t: t < 3000.0, double, z2)
    inverse = q_ref[...]
    w = dot(rhs, inverse)
    w = w + dot(rhs - dot(w, gram), inverse)
    w_ref[:, pl.ds(0, members)], w_ref[:, pl.ds(members, members)] = split(w)


def weights(z, omega, where, arrays):
    members = z.shape[0]
    vmem = pl.BlockSpec(memory_space=pltpu.VMEM)
    return pl.pallas_call(
        functools.partial(weights_kernel, where),
        in_specs=[vmem] * (2 + len(arrays)),
        out_specs=vmem,
        out_shape=jax.ShapeDtypeStruct((members, 2 * members), BF16),
        scratch_shapes=[
            pltpu.VMEM((members, 1024), F32),
            pltpu.VMEM((members, members), F32),
            pltpu.VMEM((members, members), F32),
        ],
        compiler_params=pltpu.CompilerParams(vmem_limit_bytes=24 * MIB),
        cost_estimate=pl.CostEstimate(
            flops=4000 * members**3, bytes_accessed=8 * z.size, transcendentals=0
        ),
        name="weights",
    )(z, omega, *arrays)


def apply_kernel(where, w_ref, *refs):
    parts, (out_hbm, stage, out_ref, sems) = refs[:-4], refs[-4:]
    devices = len(where)
    members = w_ref.shape[0]
    w = w_ref[...]
    copies = []
    for f in range(3):
        for half, base in enumerate(half_bases()):
            for r in range(0, STEPS, 2):
                pair = []
                for k in (r, r + 1):
                    pieces = [piece(parts, where, s, f, half, k) for s in range(devices)]
                    pair.append(jnp.concatenate(pieces + pieces, axis=0))
                both = jnp.dot(w, jnp.concatenate(pair, axis=1), preferred_element_type=F32)
                for k in range(2):
                    rows = pl.ds(base + (r + k), members, stride=8)
                    stage[f % 2, rows, :] = both[:, k * 128 : (k + 1) * 128]
        out_ref[f] = stage[f % 2].astype(BF16)
        copies.append(pltpu.make_async_copy(out_ref.at[f], out_hbm.at[f], sems.at[f]))
        copies[-1].start()
    for copy in copies:
        copy.wait()


def apply_weights(w, where, arrays):
    members = w.shape[0]
    vmem = pl.BlockSpec(memory_space=pltpu.VMEM)
    shape = (3, members * 8, 128)
    return pl.pallas_call(
        functools.partial(apply_kernel, where),
        in_specs=[vmem] * (1 + len(arrays)),
        out_specs=pl.BlockSpec(memory_space=pltpu.HBM),
        out_shape=jax.ShapeDtypeStruct(shape, BF16),
        scratch_shapes=[
            pltpu.VMEM((2, members * 8, 128), F32),
            pltpu.VMEM(shape, BF16),
            pltpu.SemaphoreType.DMA((3,)),
        ],
        compiler_params=pltpu.CompilerParams(vmem_limit_bytes=24 * MIB),
        cost_estimate=pl.CostEstimate(
            flops=12 * members * members * 1024, bytes_accessed=12 * members * 1024, transcendentals=0
        ),
        name="apply_weights",
    )(w, *arrays)


def send(x, shift):
    size = lax.axis_size("mem")
    return lax.ppermute(x, "mem", [(i, (i + shift) % size) for i in range(size)])


def body(members, obs_cells, obs_count, obs_values, obs_error, obs_noise):
    fields, count, lines, cols = members.shape
    x = members.reshape(fields, count, lines, cols // 128, 128)
    x = x.transpose(0, 1, 3, 2, 4).reshape(fields, -1, 128)
    x, first, second = edges(x, cols)
    slabs = lax.axis_size("tile") * lax.axis_size("grp")
    beyond = [(s, (s + 1 if s % 2 else s - 1) % slabs) for s in range(slabs)]
    halo_first = lax.ppermute(first, "grp", [(0, 1), (1, 0)])
    halo_second = lax.ppermute(second, ("tile", "grp"), beyond)
    inner = inner_part(x, cols)
    slots = obs_cells.shape[-1]
    obs_count, inner = lax.optimization_barrier((obs_count, inner))
    z, omega = slots_to_cells(
        obs_count,
        obs_cells.reshape(1, slots),
        obs_values.reshape(1, slots),
        obs_error.reshape(1, slots),
        obs_noise.reshape(slots, -1),
    )
    halo_first, z, omega = lax.optimization_barrier((halo_first, z, omega))
    size = lax.axis_size("mem")
    every = tuple(range(fields))
    early = side_part(inner, halo_first, False, tuple((s, every) for s in range(size)), size)
    far = size // 2
    near = [s for s in range(1, size) if s != far]
    plan = [(0, every), (far, every)] + [(s, (0,)) for s in near] + [(s, every[1:]) for s in near]
    late = side_part(inner, halo_second, True, tuple(plan), size, early)
    arrays = [early[0]]
    where = [[None] * fields for _ in range(size)]
    for k, ((shift, held), block) in enumerate(zip(plan, late)):
        arrays.append(send(block, shift) if shift else block)
        for i, f in enumerate(held):
            where[shift][f] = ((k + 1, i, 0), (k + 1, i, STEPS)) if shift else ((0, f, 0), (1, f, 0))
    needed = 3 + len(near)
    w = weights(z, omega, where, arrays[:needed])
    out = apply_weights(w, where, arrays)
    return out.reshape(fields, -1, lines, 128)


def solution(mesh):
    in_specs = (
        P(None, "mem", ("tile", "grp"), None),
        P(("tile", "grp"), "mem", None),
        P(("tile", "grp"), "mem"),
        P(("tile", "grp"), "mem", None),
        P(("tile", "grp"), "mem", None),
        P(("tile", "grp"), "mem", None, None),
    )
    out_specs = P(None, None, ("tile", "grp"), "mem")
    return jax.shard_map(body, mesh=mesh, in_specs=in_specs, out_specs=out_specs, check_vma=False)
```

```python
import functools

import jax
import jax.numpy as jnp
from jax import lax
from jax.experimental import pallas as pl
from jax.experimental.pallas import tpu as pltpu
from jax.sharding import PartitionSpec as P

STEPS = 4
F32 = jnp.float32
BF16 = jnp.bfloat16
HIGHEST = lax.Precision.HIGHEST
CH = 0.09
CU = 0.3
MIB = 1 << 20


def dot(a, b):
    return jnp.dot(a, b, preferred_element_type=F32, precision=HIGHEST)


def dot_t(a, b, precision=HIGHEST):
    return lax.dot_general(
        a, b, (((1,), (1,)), ((), ())), preferred_element_type=F32, precision=precision
    )


def edges_kernel(x_hbm, x_ref, first_ref, second_ref, sems):
    members, cols = first_ref.shape[2:]
    odd = lax.axis_index("grp")
    copies = [pltpu.make_async_copy(x_hbm.at[f], x_ref.at[f], sems.at[f]) for f in range(3)]
    for copy in copies:
        copy.start()
    for f in range(3):
        copies[f].wait()
        for out_ref, base in ((first_ref, STEPS * (1 - odd)), (second_ref, STEPS * odd)):
            for r in range(STEPS):
                for t in range(cols // 128):
                    q = x_ref[f, pl.ds(base + (t * 8 + r), members, stride=cols // 16), :]
                    out_ref[f, r, :, pl.ds(t * 128, 128)] = q.astype(BF16)


def edges(x, cols):
    members = x.shape[1] * 16 // cols
    shape = jax.ShapeDtypeStruct((3, STEPS, members, cols), BF16)
    return pl.pallas_call(
        edges_kernel,
        in_specs=[pl.BlockSpec(memory_space=pltpu.HBM)],
        out_specs=[pl.BlockSpec(memory_space=pltpu.VMEM)] * 3,
        out_shape=[jax.ShapeDtypeStruct(x.shape, F32), shape, shape],
        scratch_shapes=[pltpu.SemaphoreType.DMA((3,))],
        compiler_params=pltpu.CompilerParams(vmem_limit_bytes=16 * MIB),
        cost_estimate=pl.CostEstimate(flops=x.size, bytes_accessed=x.size * 6, transcendentals=0),
        name="edges",
    )(pltpu.with_memory_space_constraint(x, pltpu.HBM))


INNER = [(t, r) for t in range(STEPS) for r in range(t, 8 - t) if t or r in (0, 1, 6, 7)]


def advance_rows(load, store, rows):
    def north(q):
        return pltpu.roll(q, q.shape[1] - 1, axis=1)

    def south(q):
        return pltpu.roll(q, 1, axis=1)

    def terms(p):
        h, u, v = (load(f, p) for f in range(3))
        up, um = 0.25 + u, 0.25 - u
        flux = 0.5 * (u * u) + h
        quarter = 0.25 * u
        return dict(
            h=h, u=u, v=v, up=up, um=um,
            he=h * um, hw=h * up, ue=quarter - flux, uw=quarter + flux,
        )

    west, mid = terms(rows[0] - 1), terms(rows[0])
    for p in rows:
        east = terms(p + 1)
        h, u, v = mid["h"], mid["u"], mid["v"]
        vp, vm = 0.25 + v, 0.25 - v
        flux = 0.5 * (v * v) + h
        quarter = 0.25 * v
        store(0, p, (east["he"] + west["hw"]) + (north(h * vm) + south(h * vp)))
        store(1, p, (east["ue"] + west["uw"]) + (north(u) * vm + south(u) * vp) + 0.1 * v)
        store(
            2,
            p,
            (north(quarter - flux) + south(quarter + flux))
            + (east["v"] * mid["um"] + west["v"] * mid["up"])
            - 0.1 * u,
        )
        west, mid = mid, east


def inner_kernel(x_ref, inner_ref):
    members, cols = inner_ref.shape[2:]
    tiles, stride = cols // 128, cols // 16

    def group(g, _):
        part = pl.ds(pl.multiple_of(g * 8, 8), 8)
        base = pl.multiple_of(g * (8 * stride), 8 * stride)

        def load(f, p):
            q = jnp.concatenate(
                [x_ref[f, pl.ds(base + (t * 8 + p), 8, stride=stride), :] for t in range(tiles)],
                axis=1,
            )
            return q * CH + CH if f == 0 else q * CU

        for p in (0, 1, 6, 7):
            for f in range(3):
                inner_ref[f, INNER.index((0, p)), part, :] = load(f, p)
        for step in range(1, STEPS):

            def source(f, p):
                if step == 1:
                    return load(f, p)
                return inner_ref[f, INNER.index((step - 1, p)), part, :]

            def target(f, p, q):
                inner_ref[f, INNER.index((step, p)), part, :] = q

            advance_rows(source, target, range(step, 8 - step))
        return 0

    lax.fori_loop(0, members // 8, group, 0)


def inner_part(x, cols):
    members = x.shape[1] * 16 // cols
    vmem = pl.BlockSpec(memory_space=pltpu.VMEM)
    return pl.pallas_call(
        inner_kernel,
        in_specs=[vmem],
        out_specs=vmem,
        out_shape=jax.ShapeDtypeStruct((3, len(INNER), members, cols), F32),
        compiler_params=pltpu.CompilerParams(vmem_limit_bytes=32 * MIB),
        cost_estimate=pl.CostEstimate(flops=x.size * 50, bytes_accessed=x.size * 8, transcendentals=0),
        name="forecast_inner",
    )(x)


def side_kernel(second, plan, tiles, inner_ref, halo_ref, *refs):
    outs, (ping, pong, edge) = refs[-3 - len(plan) : -3], refs[-3:]
    before = refs[: -3 - len(plan)]
    members, cols = halo_ref.shape[2:]
    for f in range(3):
        for r in range(STEPS):
            q = halo_ref[f, r].astype(F32)
            edge[f, r] = q * CH + CH if f == 0 else q * CU

    def side(above):
        def first_row(t):
            return 8 - t if above else t - STEPS

        def group(g, _):
            part = pl.ds(pl.multiple_of(g * 8, 8), 8)
            for step in range(1, STEPS + 1):
                source_ref, target_ref = (ping, pong) if step % 2 else (pong, ping)

                def source(f, p):
                    if step - 1 <= p < 9 - step:
                        return inner_ref[f, INNER.index((step - 1, p)), part, :]
                    if step == 1:
                        return edge[f, p - 8 if above else p + STEPS, part, :]
                    return source_ref[f, p - first_row(step - 1), part, :]

                def target(f, p, q):
                    target_ref[f, p - first_row(step), part, :] = q

                advance_rows(source, target, range(first_row(step), first_row(step) + STEPS))
            return 0

        lax.fori_loop(0, members // 8, group, 0)

    from_above = lax.axis_index("grp") == (1 if second else 0)
    pl.when(from_above)(lambda: side(True))
    pl.when(jnp.logical_not(from_above))(lambda: side(False))
    last = ping if STEPS % 2 == 0 else pong
    rank = lax.axis_index("mem")
    for (shift, fields), out_ref in zip(plan, outs):
        base = out_ref.shape[1] - STEPS
        part = pl.ds(pl.multiple_of(lax.bitwise_xor(rank, shift) * 128, 128), 128)
        for k, f in enumerate(fields):
            if base:
                out_ref[k, :STEPS] = before[shift][f]
            for r in range(STEPS):
                q = last[f, r, :, part]
                q = q * (1.0 / CH) - 1.0 if f == 0 else q * (1.0 / CU)
                out_ref[k, base + r] = q.astype(BF16)


def side_part(inner, halo, second, plan, tiles, before=()):
    members, cols = halo.shape[2:]
    vmem = pl.BlockSpec(memory_space=pltpu.VMEM)
    rows = [STEPS if shift == 0 or not second else 2 * STEPS for shift, _ in plan]
    return pl.pallas_call(
        functools.partial(side_kernel, second, plan, tiles),
        in_specs=[vmem] * (2 + len(before)),
        out_specs=[vmem] * len(plan),
        out_shape=[
            jax.ShapeDtypeStruct((len(fields), n, members, 128), BF16)
            for n, (_, fields) in zip(rows, plan)
        ],
        scratch_shapes=[pltpu.VMEM((3, STEPS, members, cols), F32)] * 3,
        compiler_params=pltpu.CompilerParams(vmem_limit_bytes=24 * MIB),
        cost_estimate=pl.CostEstimate(
            flops=halo.size * 160, bytes_accessed=halo.size * 16, transcendentals=0
        ),
        name="forecast_second" if second else "forecast_first",
    )(inner, halo, *before)


def slots_kernel(count_ref, cells_ref, values_ref, error_ref, noise_ref, z_ref, omega_ref, lhs):
    slots = cells_ref.shape[1]
    members = noise_ref.shape[1]
    error = error_ref[...]
    live = lax.broadcasted_iota(jnp.int32, (1, slots), 1) < count_ref[0, 0]
    weight = jnp.where(live, 1.0 / (error * error), 0.0)
    rows = members + 16

    def put(at, size, cols, value):
        high = value.astype(BF16)
        rest = value - high.astype(F32)
        middle = rest.astype(BF16)
        low = (rest - middle.astype(F32)).astype(BF16)
        for k, q in enumerate((high, middle, low)):
            lhs[pl.ds(k * rows + at, size), cols] = q

    for b in range(slots // 128):
        part = pl.ds(b * 128, 128)
        lane = slice(b * 128, (b + 1) * 128)
        innovation = values_ref[:, part] + error[:, lane] * noise_ref[part, :].T
        put(0, members, part, weight[:, lane] * innovation)
    put(members, 16, pl.ds(0, slots), jnp.broadcast_to(weight, (16, slots)))
    block = 256
    cells = cells_ref[...]
    for b in range(z_ref.shape[1] // block):
        ids = lax.broadcasted_iota(jnp.int32, (block, slots), 0) + b * block
        chosen = jnp.where(ids == cells, 1.0, 0.0).astype(BF16)
        total = lax.dot_general(
            lhs[...], chosen, (((1,), (1,)), ((), ())), preferred_element_type=F32
        )
        total = total[:rows] + (total[rows : 2 * rows] + total[2 * rows :])
        part = pl.ds(b * block, block)
        z_ref[:, part] = total[:members]
        omega_ref[:, part] = total[members : members + 8]


def slots_to_cells(count, cells, values, error, noise):
    slots, members = noise.shape
    vmem = pl.BlockSpec(memory_space=pltpu.VMEM)
    return pl.pallas_call(
        slots_kernel,
        in_specs=[pl.BlockSpec(memory_space=pltpu.SMEM)] + [vmem] * 4,
        out_specs=[vmem, vmem],
        out_shape=[
            jax.ShapeDtypeStruct((members, 1024), F32),
            jax.ShapeDtypeStruct((8, 1024), F32),
        ],
        scratch_shapes=[pltpu.VMEM((3 * (members + 16), slots), BF16)],
        compiler_params=pltpu.CompilerParams(vmem_limit_bytes=32 * MIB),
        cost_estimate=pl.CostEstimate(
            flops=4 * members * slots * 1024, bytes_accessed=8 * noise.size, transcendentals=0
        ),
        name="slots_to_cells",
    )(count, cells, values, error, noise)


def split(a):
    high = a.astype(BF16)
    return high, (a - high.astype(F32)).astype(BF16)


def half_bases():
    odd = lax.axis_index("grp")
    return STEPS * (1 - odd), STEPS * odd


def piece(refs, where, s, f, half, r):
    array, field, row = where[s][f][half]
    return refs[array][field, row + r]


def weights_kernel(where, z_ref, omega_ref, *refs):
    parts, (w_ref, x_ref, t_ref, q_ref) = refs[:-4], refs[-4:]
    devices = len(where)
    size = parts[0].shape[2]
    members = size * devices
    for half, base in enumerate(half_bases()):
        for r in range(STEPS):
            lanes = pl.ds(pl.multiple_of((base + r) * 128, 128), 128)
            for s in range(devices):
                x_ref[pl.ds(s * size, size), lanes] = piece(parts, where, s, 0, half, r).astype(F32)
    x = x_ref[...]
    mean = jnp.sum(x, axis=0, keepdims=True) * (1.0 / members)
    x = x - mean
    omega = omega_ref[pl.ds(0, 1), :]
    left_high, left_low = split(jnp.concatenate([x * omega, z_ref[...] - omega * mean], axis=0))
    high, low = split(x)
    both = dot_t(left_high, high, None) + (
        dot_t(left_high, low, None) + dot_t(left_low, high, None)
    )
    shape = (members, members)
    down = lax.broadcasted_iota(jnp.int32, shape, 0)
    across = lax.broadcasted_iota(jnp.int32, shape, 1)
    eye = jnp.where(down == across, 1.0, 0.0)
    rank = lax.axis_index("mem")
    member = lax.bitwise_xor(across // size, rank) * size + lax.rem(across, size)
    own = jnp.where(down == member, 1.0, 0.0)
    diagonal = members - 1.0
    gram = both[:members]
    rhs = both[members:] + diagonal * own
    square = dot(gram, gram)
    gram = gram + diagonal * eye
    top = jnp.sqrt(jnp.sqrt(jnp.sum(square * square)))
    low = 0.98 * diagonal
    high = 1.01 * (diagonal + top)
    inv = 1.0 / (high - low)
    z = (high + low) * inv
    alpha = (high + low - 2.0 * diagonal) * inv
    beta = 2.0 * inv
    less = gram - diagonal * eye
    t1 = alpha * eye - beta * less
    t2 = (2.0 * alpha * alpha - 1.0) * eye - (4.0 * alpha * beta) * less + (2.0 * beta * beta) * square
    z2 = 2.0 * z * z - 1.0
    t_ref[...] = t2
    q_ref[...] = (2.0 / (high + low)) * (2.0 * z / z2) * (z * eye + t1)

    def double(t):
        cheb, q = t_ref[...], q_ref[...]
        after = 2.0 * t * t - 1.0
        q_ref[...] = (2.0 * t / after) * (t * q + dot(q, cheb))
        t_ref[...] = 2.0 * dot(cheb, cheb) - eye
        return after

    lax.while_loop(lambda t: t < 3000.0, double, z2)
    inverse = q_ref[...]
    w = dot(rhs, inverse)
    w = w + dot(rhs - dot(w, gram), inverse)
    w_ref[:, pl.ds(0, members)], w_ref[:, pl.ds(members, members)] = split(w)


def weights(z, omega, where, arrays):
    members = z.shape[0]
    vmem = pl.BlockSpec(memory_space=pltpu.VMEM)
    return pl.pallas_call(
        functools.partial(weights_kernel, where),
        in_specs=[vmem] * (2 + len(arrays)),
        out_specs=vmem,
        out_shape=jax.ShapeDtypeStruct((members, 2 * members), BF16),
        scratch_shapes=[
            pltpu.VMEM((members, 1024), F32),
            pltpu.VMEM((members, members), F32),
            pltpu.VMEM((members, members), F32),
        ],
        compiler_params=pltpu.CompilerParams(vmem_limit_bytes=24 * MIB),
        cost_estimate=pl.CostEstimate(
            flops=4000 * members**3, bytes_accessed=8 * z.size, transcendentals=0
        ),
        name="weights",
    )(z, omega, *arrays)


def apply_kernel(where, w_ref, *refs):
    parts, (out_hbm, stage, out_ref, sems) = refs[:-4], refs[-4:]
    devices = len(where)
    members = w_ref.shape[0]
    w = w_ref[...]
    copies = []
    for f in range(3):
        for half, base in enumerate(half_bases()):
            for r in range(0, STEPS, 2):
                pair = []
                for k in (r, r + 1):
                    pieces = [piece(parts, where, s, f, half, k) for s in range(devices)]
                    pair.append(jnp.concatenate(pieces + pieces, axis=0))
                both = jnp.dot(w, jnp.concatenate(pair, axis=1), preferred_element_type=F32)
                for k in range(2):
                    rows = pl.ds(base + (r + k), members, stride=8)
                    stage[f % 2, rows, :] = both[:, k * 128 : (k + 1) * 128]
        out_ref[f] = stage[f % 2].astype(BF16)
        copies.append(pltpu.make_async_copy(out_ref.at[f], out_hbm.at[f], sems.at[f]))
        copies[-1].start()
    for copy in copies:
        copy.wait()


def apply_weights(w, where, arrays):
    members = w.shape[0]
    vmem = pl.BlockSpec(memory_space=pltpu.VMEM)
    shape = (3, members * 8, 128)
    return pl.pallas_call(
        functools.partial(apply_kernel, where),
        in_specs=[vmem] * (1 + len(arrays)),
        out_specs=pl.BlockSpec(memory_space=pltpu.HBM),
        out_shape=jax.ShapeDtypeStruct(shape, BF16),
        scratch_shapes=[
            pltpu.VMEM((2, members * 8, 128), F32),
            pltpu.VMEM(shape, BF16),
            pltpu.SemaphoreType.DMA((3,)),
        ],
        compiler_params=pltpu.CompilerParams(vmem_limit_bytes=24 * MIB),
        cost_estimate=pl.CostEstimate(
            flops=12 * members * members * 1024, bytes_accessed=12 * members * 1024, transcendentals=0
        ),
        name="apply_weights",
    )(w, *arrays)


def send(x, shift):
    size = lax.axis_size("mem")
    return lax.ppermute(x, "mem", [(i, i ^ shift) for i in range(size)])


def body(members, obs_cells, obs_count, obs_values, obs_error, obs_noise):
    fields, count, lines, cols = members.shape
    x = members.reshape(fields, count, lines, cols // 128, 128)
    x = x.transpose(0, 1, 3, 2, 4).reshape(fields, -1, 128)
    x, first, second = edges(x, cols)
    slabs = lax.axis_size("tile") * lax.axis_size("grp")
    beyond = [(s, (s + 1 if s % 2 else s - 1) % slabs) for s in range(slabs)]
    halo_first = lax.ppermute(first, "grp", [(0, 1), (1, 0)])
    halo_second = lax.ppermute(second, ("tile", "grp"), beyond)
    inner = inner_part(x, cols)
    slots = obs_cells.shape[-1]
    obs_count, inner = lax.optimization_barrier((obs_count, inner))
    z, omega = slots_to_cells(
        obs_count,
        obs_cells.reshape(1, slots),
        obs_values.reshape(1, slots),
        obs_error.reshape(1, slots),
        obs_noise.reshape(slots, -1),
    )
    halo_first, z, omega = lax.optimization_barrier((halo_first, z, omega))
    size = lax.axis_size("mem")
    every = tuple(range(fields))
    early = side_part(inner, halo_first, False, tuple((s, every) for s in range(size)), size)
    far = size // 2
    near = [s for s in range(1, size) if s != far]
    plan = [(0, every), (far, every)] + [(s, (0,)) for s in near] + [(s, every[1:]) for s in near]
    late = side_part(inner, halo_second, True, tuple(plan), size, early)
    arrays = [early[0]]
    where = [[None] * fields for _ in range(size)]
    for k, ((shift, held), block) in enumerate(zip(plan, late)):
        arrays.append(send(block, shift) if shift else block)
        for i, f in enumerate(held):
            where[shift][f] = ((k + 1, i, 0), (k + 1, i, STEPS)) if shift else ((0, f, 0), (1, f, 0))
    needed = 3 + len(near)
    w = weights(z, omega, where, arrays[:needed])
    out = apply_weights(w, where, arrays)
    return out.reshape(fields, -1, lines, 128)


def solution(mesh):
    in_specs = (
        P(None, "mem", ("tile", "grp"), None),
        P(("tile", "grp"), "mem", None),
        P(("tile", "grp"), "mem"),
        P(("tile", "grp"), "mem", None),
        P(("tile", "grp"), "mem", None),
        P(("tile", "grp"), "mem", None, None),
    )
    out_specs = P(None, None, ("tile", "grp"), "mem")
    return jax.shard_map(body, mesh=mesh, in_specs=in_specs, out_specs=out_specs, check_vma=False)
```

```python
import functools

import jax
import jax.numpy as jnp
from jax import lax
from jax.experimental import pallas as pl
from jax.experimental.pallas import tpu as pltpu
from jax.sharding import PartitionSpec as P

STEPS = 4
F32 = jnp.float32
BF16 = jnp.bfloat16
HIGHEST = lax.Precision.HIGHEST
CH = 0.09
CU = 0.3
MIB = 1 << 20


def dot(a, b):
    return jnp.dot(a, b, preferred_element_type=F32, precision=HIGHEST)


def dot_t(a, b, precision=HIGHEST):
    return lax.dot_general(
        a, b, (((1,), (1,)), ((), ())), preferred_element_type=F32, precision=precision
    )


def edges_kernel(x_hbm, x_ref, first_ref, *refs):
    seconds, sems = refs[:-1], refs[-1]
    members, cols = first_ref.shape[2:]
    part = members // len(seconds)
    outs = [(first_ref, 0, 0)] + [(ref, 1, k * part) for k, ref in enumerate(seconds)]
    odd = lax.axis_index("grp")
    copies = [pltpu.make_async_copy(x_hbm.at[f], x_ref.at[f], sems.at[f]) for f in range(3)]
    for copy in copies:
        copy.start()
    for f in range(3):
        copies[f].wait()
        for out_ref, beyond, begin in outs:
            base = STEPS * odd if beyond else STEPS * (1 - odd)
            for r in range(STEPS):
                for t in range(cols // 128):
                    at = base + (begin * (cols // 16) + t * 8 + r)
                    q = x_ref[f, pl.ds(at, out_ref.shape[2], stride=cols // 16), :]
                    out_ref[f, r, :, pl.ds(t * 128, 128)] = q.astype(BF16)


def edges(x, cols):
    members = x.shape[1] * 16 // cols
    shape = jax.ShapeDtypeStruct((3, STEPS, members, cols), BF16)
    half = jax.ShapeDtypeStruct((3, STEPS, members // 2, cols), BF16)
    return pl.pallas_call(
        edges_kernel,
        in_specs=[pl.BlockSpec(memory_space=pltpu.HBM)],
        out_specs=[pl.BlockSpec(memory_space=pltpu.VMEM)] * 4,
        out_shape=[jax.ShapeDtypeStruct(x.shape, F32), shape, half, half],
        scratch_shapes=[pltpu.SemaphoreType.DMA((3,))],
        compiler_params=pltpu.CompilerParams(vmem_limit_bytes=16 * MIB),
        cost_estimate=pl.CostEstimate(flops=x.size, bytes_accessed=x.size * 6, transcendentals=0),
        name="edges",
    )(pltpu.with_memory_space_constraint(x, pltpu.HBM))


INNER = [(t, r) for t in range(STEPS) for r in range(t, 8 - t) if t or r in (0, 1, 6, 7)]


def advance_rows(load, store, rows):
    def north(q):
        return pltpu.roll(q, q.shape[1] - 1, axis=1)

    def south(q):
        return pltpu.roll(q, 1, axis=1)

    def terms(p):
        h, u, v = (load(f, p) for f in range(3))
        up, um = 0.25 + u, 0.25 - u
        flux = 0.5 * (u * u) + h
        quarter = 0.25 * u
        return dict(
            h=h, u=u, v=v, up=up, um=um,
            he=h * um, hw=h * up, ue=quarter - flux, uw=quarter + flux,
        )

    west, mid = terms(rows[0] - 1), terms(rows[0])
    for p in rows:
        east = terms(p + 1)
        h, u, v = mid["h"], mid["u"], mid["v"]
        vp, vm = 0.25 + v, 0.25 - v
        flux = 0.5 * (v * v) + h
        quarter = 0.25 * v
        store(0, p, (east["he"] + west["hw"]) + (north(h * vm) + south(h * vp)))
        store(1, p, (east["ue"] + west["uw"]) + (north(u) * vm + south(u) * vp) + 0.1 * v)
        store(
            2,
            p,
            (north(quarter - flux) + south(quarter + flux))
            + (east["v"] * mid["um"] + west["v"] * mid["up"])
            - 0.1 * u,
        )
        west, mid = mid, east


def inner_kernel(x_ref, inner_ref):
    members, cols = inner_ref.shape[2:]
    tiles, stride = cols // 128, cols // 16

    def group(g, _):
        part = pl.ds(pl.multiple_of(g * 8, 8), 8)
        base = pl.multiple_of(g * (8 * stride), 8 * stride)

        def load(f, p):
            q = jnp.concatenate(
                [x_ref[f, pl.ds(base + (t * 8 + p), 8, stride=stride), :] for t in range(tiles)],
                axis=1,
            )
            return q * CH + CH if f == 0 else q * CU

        for p in (0, 1, 6, 7):
            for f in range(3):
                inner_ref[f, INNER.index((0, p)), part, :] = load(f, p)
        for step in range(1, STEPS):

            def source(f, p):
                if step == 1:
                    return load(f, p)
                return inner_ref[f, INNER.index((step - 1, p)), part, :]

            def target(f, p, q):
                inner_ref[f, INNER.index((step, p)), part, :] = q

            advance_rows(source, target, range(step, 8 - step))
        return 0

    lax.fori_loop(0, members // 8, group, 0)


def inner_part(x, cols):
    members = x.shape[1] * 16 // cols
    vmem = pl.BlockSpec(memory_space=pltpu.VMEM)
    return pl.pallas_call(
        inner_kernel,
        in_specs=[vmem],
        out_specs=vmem,
        out_shape=jax.ShapeDtypeStruct((3, len(INNER), members, cols), F32),
        compiler_params=pltpu.CompilerParams(vmem_limit_bytes=32 * MIB),
        cost_estimate=pl.CostEstimate(flops=x.size * 50, bytes_accessed=x.size * 8, transcendentals=0),
        name="forecast_inner",
    )(x)


def side_kernel(second, plan, tiles, begin, inner_ref, halo_ref, *refs):
    count = max(1, len(plan))
    outs, (ping, pong, edge) = refs[-3 - count : -3], refs[-3:]
    before = refs[: -3 - count]
    if begin:
        before, other = before[:-1], before[-1]
    members, cols = halo_ref.shape[2:]
    for f in range(3):
        for r in range(STEPS):
            q = halo_ref[f, r].astype(F32)
            edge[f, r] = q * CH + CH if f == 0 else q * CU

    def side(above):
        def first_row(t):
            return 8 - t if above else t - STEPS

        def group(g, _):
            part = pl.ds(pl.multiple_of(g * 8, 8), 8)
            held = pl.ds(pl.multiple_of(begin + g * 8, 8), 8)
            for step in range(1, STEPS + 1):
                source_ref, target_ref = (ping, pong) if step % 2 else (pong, ping)

                def source(f, p):
                    if step - 1 <= p < 9 - step:
                        return inner_ref[f, INNER.index((step - 1, p)), held, :]
                    if step == 1:
                        return edge[f, p - 8 if above else p + STEPS, part, :]
                    return source_ref[f, p - first_row(step - 1), part, :]

                def target(f, p, q):
                    target_ref[f, p - first_row(step), part, :] = q

                advance_rows(source, target, range(first_row(step), first_row(step) + STEPS))
            return 0

        lax.fori_loop(0, members // 8, group, 0)

    from_above = lax.axis_index("grp") == (1 if second else 0)
    pl.when(from_above)(lambda: side(True))
    pl.when(jnp.logical_not(from_above))(lambda: side(False))
    last = ping if STEPS % 2 == 0 else pong
    if not plan:
        outs[0][...] = last[...]
        return
    sources = [(last, pl.ds(begin, members))] + ([(other, pl.ds(0, begin))] if begin else [])
    rank = lax.axis_index("mem")
    for (shift, fields), out_ref in zip(plan, outs):
        base = out_ref.shape[1] - STEPS
        part = pl.ds(pl.multiple_of(lax.bitwise_xor(rank, shift) * 128, 128), 128)
        for k, f in enumerate(fields):
            if base:
                out_ref[k, :STEPS] = before[shift][f]
            for r in range(STEPS):
                for ref, place in sources:
                    q = ref[f, r, :, part]
                    q = q * (1.0 / CH) - 1.0 if f == 0 else q * (1.0 / CU)
                    out_ref[k, base + r, place, :] = q.astype(BF16)


def side_part(inner, halo, second, plan, tiles, before=(), begin=0):
    members, cols = halo.shape[2:]
    vmem = pl.BlockSpec(memory_space=pltpu.VMEM)
    rows = [STEPS if shift == 0 or not second else 2 * STEPS for shift, _ in plan]
    return pl.pallas_call(
        functools.partial(side_kernel, second, plan, tiles, begin),
        in_specs=[vmem] * (2 + len(before)),
        out_specs=[vmem] * max(1, len(plan)),
        out_shape=[
            jax.ShapeDtypeStruct((len(fields), n, begin + members, 128), BF16)
            for n, (_, fields) in zip(rows, plan)
        ]
        or [jax.ShapeDtypeStruct((3, STEPS, members, cols), F32)],
        scratch_shapes=[pltpu.VMEM((3, STEPS, members, cols), F32)] * 3,
        compiler_params=pltpu.CompilerParams(vmem_limit_bytes=24 * MIB),
        cost_estimate=pl.CostEstimate(
            flops=halo.size * 160, bytes_accessed=halo.size * 16, transcendentals=0
        ),
        name="forecast_second" if second else "forecast_first",
    )(inner, halo, *before)


def slots_kernel(count_ref, cells_ref, values_ref, error_ref, noise_ref, z_ref, omega_ref, lhs):
    slots = cells_ref.shape[1]
    members = noise_ref.shape[1]
    error = error_ref[...]
    live = lax.broadcasted_iota(jnp.int32, (1, slots), 1) < count_ref[0, 0]
    weight = jnp.where(live, 1.0 / (error * error), 0.0)
    rows = members + 16

    def put(at, size, cols, value):
        high = value.astype(BF16)
        rest = value - high.astype(F32)
        middle = rest.astype(BF16)
        low = (rest - middle.astype(F32)).astype(BF16)
        for k, q in enumerate((high, middle, low)):
            lhs[pl.ds(k * rows + at, size), cols] = q

    for b in range(slots // 128):
        part = pl.ds(b * 128, 128)
        lane = slice(b * 128, (b + 1) * 128)
        innovation = values_ref[:, part] + error[:, lane] * noise_ref[part, :].T
        put(0, members, part, weight[:, lane] * innovation)
    put(members, 16, pl.ds(0, slots), jnp.broadcast_to(weight, (16, slots)))
    block = 256
    cells = cells_ref[...]
    for b in range(z_ref.shape[1] // block):
        ids = lax.broadcasted_iota(jnp.int32, (block, slots), 0) + b * block
        chosen = jnp.where(ids == cells, 1.0, 0.0).astype(BF16)
        total = lax.dot_general(
            lhs[...], chosen, (((1,), (1,)), ((), ())), preferred_element_type=F32
        )
        total = total[:rows] + (total[rows : 2 * rows] + total[2 * rows :])
        part = pl.ds(b * block, block)
        z_ref[:, part] = total[:members]
        omega_ref[:, part] = total[members : members + 8]


def slots_to_cells(count, cells, values, error, noise):
    slots, members = noise.shape
    vmem = pl.BlockSpec(memory_space=pltpu.VMEM)
    return pl.pallas_call(
        slots_kernel,
        in_specs=[pl.BlockSpec(memory_space=pltpu.SMEM)] + [vmem] * 4,
        out_specs=[vmem, vmem],
        out_shape=[
            jax.ShapeDtypeStruct((members, 1024), F32),
            jax.ShapeDtypeStruct((8, 1024), F32),
        ],
        scratch_shapes=[pltpu.VMEM((3 * (members + 16), slots), BF16)],
        compiler_params=pltpu.CompilerParams(vmem_limit_bytes=32 * MIB),
        cost_estimate=pl.CostEstimate(
            flops=4 * members * slots * 1024, bytes_accessed=8 * noise.size, transcendentals=0
        ),
        name="slots_to_cells",
    )(count, cells, values, error, noise)


def split(a):
    high = a.astype(BF16)
    return high, (a - high.astype(F32)).astype(BF16)


def half_bases():
    odd = lax.axis_index("grp")
    return STEPS * (1 - odd), STEPS * odd


def piece(refs, where, s, f, half, r):
    array, field, row = where[s][f][half]
    return refs[array][field, row + r]


def weights_kernel(where, z_ref, omega_ref, *refs):
    parts, (w_ref, x_ref, t_ref, q_ref) = refs[:-4], refs[-4:]
    devices = len(where)
    size = parts[0].shape[2]
    members = size * devices
    for half, base in enumerate(half_bases()):
        for r in range(STEPS):
            lanes = pl.ds(pl.multiple_of((base + r) * 128, 128), 128)
            for s in range(devices):
                x_ref[pl.ds(s * size, size), lanes] = piece(parts, where, s, 0, half, r).astype(F32)
    x = x_ref[...]
    mean = jnp.sum(x, axis=0, keepdims=True) * (1.0 / members)
    x = x - mean
    omega = omega_ref[pl.ds(0, 1), :]
    left_high, left_low = split(jnp.concatenate([x * omega, z_ref[...] - omega * mean], axis=0))
    high, low = split(x)
    both = dot_t(left_high, high, None) + (
        dot_t(left_high, low, None) + dot_t(left_low, high, None)
    )
    shape = (members, members)
    down = lax.broadcasted_iota(jnp.int32, shape, 0)
    across = lax.broadcasted_iota(jnp.int32, shape, 1)
    eye = jnp.where(down == across, 1.0, 0.0)
    rank = lax.axis_index("mem")
    member = lax.bitwise_xor(across // size, rank) * size + lax.rem(across, size)
    own = jnp.where(down == member, 1.0, 0.0)
    diagonal = members - 1.0
    gram = both[:members]
    rhs = both[members:] + diagonal * own
    square = dot(gram, gram)
    gram = gram + diagonal * eye
    top = jnp.sqrt(jnp.sqrt(jnp.sum(square * square)))
    low = 0.98 * diagonal
    high = 1.01 * (diagonal + top)
    inv = 1.0 / (high - low)
    z = (high + low) * inv
    alpha = (high + low - 2.0 * diagonal) * inv
    beta = 2.0 * inv
    less = gram - diagonal * eye
    t1 = alpha * eye - beta * less
    t2 = (2.0 * alpha * alpha - 1.0) * eye - (4.0 * alpha * beta) * less + (2.0 * beta * beta) * square
    z2 = 2.0 * z * z - 1.0
    t_ref[...] = t2
    q_ref[...] = (2.0 / (high + low)) * (2.0 * z / z2) * (z * eye + t1)

    def double(t):
        cheb, q = t_ref[...], q_ref[...]
        after = 2.0 * t * t - 1.0
        q_ref[...] = (2.0 * t / after) * (t * q + dot(q, cheb))
        t_ref[...] = 2.0 * dot(cheb, cheb) - eye
        return after

    lax.while_loop(lambda t: t < 3000.0, double, z2)
    inverse = q_ref[...]
    w = dot(rhs, inverse)
    w = w + dot(rhs - dot(w, gram), inverse)
    w_ref[:, pl.ds(0, members)], w_ref[:, pl.ds(members, members)] = split(w)


def weights(z, omega, where, arrays):
    members = z.shape[0]
    vmem = pl.BlockSpec(memory_space=pltpu.VMEM)
    return pl.pallas_call(
        functools.partial(weights_kernel, where),
        in_specs=[vmem] * (2 + len(arrays)),
        out_specs=vmem,
        out_shape=jax.ShapeDtypeStruct((members, 2 * members), BF16),
        scratch_shapes=[
            pltpu.VMEM((members, 1024), F32),
            pltpu.VMEM((members, members), F32),
            pltpu.VMEM((members, members), F32),
        ],
        compiler_params=pltpu.CompilerParams(vmem_limit_bytes=24 * MIB),
        cost_estimate=pl.CostEstimate(
            flops=4000 * members**3, bytes_accessed=8 * z.size, transcendentals=0
        ),
        name="weights",
    )(z, omega, *arrays)


def apply_kernel(where, w_ref, *refs):
    parts, (out_hbm, stage, out_ref, sems) = refs[:-4], refs[-4:]
    devices = len(where)
    members = w_ref.shape[0]
    w = w_ref[...]
    copies = []
    for f in range(3):
        for half, base in enumerate(half_bases()):
            for r in range(0, STEPS, 2):
                pair = []
                for k in (r, r + 1):
                    pieces = [piece(parts, where, s, f, half, k) for s in range(devices)]
                    pair.append(jnp.concatenate(pieces + pieces, axis=0))
                both = jnp.dot(w, jnp.concatenate(pair, axis=1), preferred_element_type=F32)
                for k in range(2):
                    rows = pl.ds(base + (r + k), members, stride=8)
                    stage[f % 2, rows, :] = both[:, k * 128 : (k + 1) * 128]
        out_ref[f] = stage[f % 2].astype(BF16)
        copies.append(pltpu.make_async_copy(out_ref.at[f], out_hbm.at[f], sems.at[f]))
        copies[-1].start()
    for copy in copies:
        copy.wait()


def apply_weights(w, where, arrays):
    members = w.shape[0]
    vmem = pl.BlockSpec(memory_space=pltpu.VMEM)
    shape = (3, members * 8, 128)
    return pl.pallas_call(
        functools.partial(apply_kernel, where),
        in_specs=[vmem] * (1 + len(arrays)),
        out_specs=pl.BlockSpec(memory_space=pltpu.HBM),
        out_shape=jax.ShapeDtypeStruct(shape, BF16),
        scratch_shapes=[
            pltpu.VMEM((2, members * 8, 128), F32),
            pltpu.VMEM(shape, BF16),
            pltpu.SemaphoreType.DMA((3,)),
        ],
        compiler_params=pltpu.CompilerParams(vmem_limit_bytes=24 * MIB),
        cost_estimate=pl.CostEstimate(
            flops=12 * members * members * 1024, bytes_accessed=12 * members * 1024, transcendentals=0
        ),
        name="apply_weights",
    )(w, *arrays)


def send(x, shift):
    size = lax.axis_size("mem")
    return lax.ppermute(x, "mem", [(i, i ^ shift) for i in range(size)])


def body(members, obs_cells, obs_count, obs_values, obs_error, obs_noise):
    fields, count, lines, cols = members.shape
    x = members.reshape(fields, count, lines, cols // 128, 128)
    x = x.transpose(0, 1, 3, 2, 4).reshape(fields, -1, 128)
    x, first, *seconds = edges(x, cols)
    slabs = lax.axis_size("tile") * lax.axis_size("grp")
    beyond = [(s, (s + 1 if s % 2 else s - 1) % slabs) for s in range(slabs)]
    halo_first = lax.ppermute(first, "grp", [(0, 1), (1, 0)])
    halo_seconds = [lax.ppermute(second, ("tile", "grp"), beyond) for second in seconds]
    inner = inner_part(x, cols)
    slots = obs_cells.shape[-1]
    obs_count, inner = lax.optimization_barrier((obs_count, inner))
    z, omega = slots_to_cells(
        obs_count,
        obs_cells.reshape(1, slots),
        obs_values.reshape(1, slots),
        obs_error.reshape(1, slots),
        obs_noise.reshape(slots, -1),
    )
    halo_first, z, omega = lax.optimization_barrier((halo_first, z, omega))
    size = lax.axis_size("mem")
    every = tuple(range(fields))
    early = side_part(inner, halo_first, False, tuple((s, every) for s in range(size)), size)
    far = size // 2
    near = [s for s in range(1, size) if s != far]
    plan = [(0, every), (far, every)] + [(s, (0,)) for s in near] + [(s, every[1:]) for s in near]
    half = count // 2
    halo_seconds[0], early = lax.optimization_barrier((halo_seconds[0], early))
    (rows,) = side_part(inner, halo_seconds[0], True, (), size)
    late = side_part(inner, halo_seconds[1], True, tuple(plan), size, [*early, rows], half)
    arrays = [early[0]]
    where = [[None] * fields for _ in range(size)]
    for k, ((shift, held), block) in enumerate(zip(plan, late)):
        arrays.append(send(block, shift) if shift else block)
        for i, f in enumerate(held):
            where[shift][f] = ((k + 1, i, 0), (k + 1, i, STEPS)) if shift else ((0, f, 0), (1, f, 0))
    needed = 3 + len(near)
    w = weights(z, omega, where, arrays[:needed])
    out = apply_weights(w, where, arrays)
    return out.reshape(fields, -1, lines, 128)


def solution(mesh):
    in_specs = (
        P(None, "mem", ("tile", "grp"), None),
        P(("tile", "grp"), "mem", None),
        P(("tile", "grp"), "mem"),
        P(("tile", "grp"), "mem", None),
        P(("tile", "grp"), "mem", None),
        P(("tile", "grp"), "mem", None, None),
    )
    out_specs = P(None, None, ("tile", "grp"), "mem")
    return jax.shard_map(body, mesh=mesh, in_specs=in_specs, out_specs=out_specs, check_vma=False)
```
